32 devices in a mesh: dp: 8 (over z, x), ctx: 4 (over y, core).
Axes of the slice: x: 2, y: 2, z: 4, core: 2. Of those that a mesh axis runs over, the one named last changes fastest.
Arguments:
- inputs: bfloat16 [512, 16, 1024], P('ctx', 'dp'), may hold values from -6 to 6
- cotangent: bfloat16 [512, 16, 1024], P('ctx', 'dp'), may hold values from -6 to 6
- lengths: int32 [16], P('dp'), may hold values from 128 to 512, as said below
- block_order: int32 [8], replicated, may hold values from 0 to 7, as said below
- norm_gain: bfloat16 [1024], P('dp'), may hold values from 0.5 to 1.5
- norm_bias: bfloat16 [1024], P('dp'), may hold values from -1.75 to 1.75
- attend_weight: bfloat16 [1024, 3072], P('dp'), may hold values from -0.1875 to 0.1875
- attend_bias: bfloat16 [3072], P('dp'), may hold values from -3 to 3
- dense_weight: bfloat16 [1024, 1024], P('dp'), may hold values from -6 to 6
- dense_bias: bfloat16 [1024], P('dp'), may hold values from -3 to 3
- up_weight: bfloat16 [1024, 4096], P('dp'), may hold values from -0.1875 to 0.1875
- up_bias: bfloat16 [4096], P('dp'), may hold values from -3 to 3
- down_weight: bfloat16 [4096, 1024], P('dp'), may hold values from -0.09375 to 0.09375
- down_bias: bfloat16 [1024], P('dp'), may hold values from -3 to 3
Outputs:
- output: bfloat16 [512, 16, 1024], P('ctx', 'dp')
- input_grad: bfloat16 [512, 16, 1024], P('ctx', 'dp')
- grad_norm_gain: float32 [1024], P('dp')
- grad_norm_bias: float32 [1024], P('dp')
- grad_attend_weight: float32 [1024, 3072], P('dp')
- grad_attend_bias: float32 [3072], P('dp')
- grad_dense_weight: float32 [1024, 1024], P('dp')
- grad_dense_bias: float32 [1024], P('dp')
- grad_up_weight: float32 [1024, 4096], P('dp')
- grad_up_bias: float32 [4096], P('dp')
- grad_down_weight: float32 [4096, 1024], P('dp')
- grad_down_bias: float32 [1024], P('dp')
The draws below stay inside these ranges and needn't reach their ends.
Inputs may be any that keep to these rules, and one draw needn't show every extreme that they name: Slots of sequence s whose position is lengths[s] or more are padding; in every draw some sequence has exactly 512 valid slots and some exactly 128. Each of 0 to 7 appears once, and block_order[2 c] + block_order[2 c + 1] = 7 for every c.
All inputs are finite; a program needn't handle non-finite values.
Results may differ from the reference program's by a relative error of at most 0.018.
Values may be sent and summed in bfloat16 or wider, within the bound.
No kernel may reach another device: no remote copies, remote signals or barrier semaphores. Data moves between devices by JAX's collectives and lax.ppermute only.
A program may use at most 320 MiB of HBM per device.

```python
import math
import jax
import jax.numpy as jnp
from jax import lax

D = 1024
FF = 4096
HEADS = 16
HEAD_DIM = 64
ROT = 16
SLOTS = 512
SEQS = 16
BLK = 64
NBLK = 8


def draw_lengths(key, part):
    first = jax.random.fold_in(key, 11)
    second = jax.random.fold_in(key, 12)
    base = jax.random.randint(first, (SEQS,), SLOTS // 4, SLOTS + 1, dtype=jnp.int32)
    order = jax.random.permutation(second, SEQS)
    base = base.at[order[0]].set(SLOTS)
    base = base.at[order[1]].set(SLOTS // 4)
    return base.astype(jnp.int32)


def draw_block_order(key, part):
    chosen = jax.random.permutation(jax.random.fold_in(key, 21), NBLK // 2).astype(jnp.int32)
    late = NBLK - 1 - chosen
    return jnp.stack([chosen, late], axis=1).reshape(NBLK).astype(jnp.int32)


def level_of(own_key, shape, pieces, least, largest):
    level = 1.0
    for axis_at, shards_of in pieces:
        draws = jax.random.uniform(jax.random.fold_in(jax.random.fold_in(own_key, 6), axis_at), (shards_of,), jnp.float32, least / len(pieces), largest / len(pieces))
        level = level * jnp.repeat(jnp.exp(draws), shape[axis_at] // shards_of).reshape((-1,) + (1,) * (len(shape) - 1 - axis_at))
    return level


def scatter_about(rng, shape, deviation, limit, pieces=(), kind=jnp.bfloat16):
    factor_of = level_of(rng, shape, pieces, -0.22, 0.18) if pieces else 1.0
    values = jax.random.normal(rng, shape, jnp.float32) * deviation * factor_of
    return jnp.minimum(jnp.maximum(values, -limit), limit).astype(kind)


def setup_inputs(seed: int = 0) -> dict:
    arg_keys = jax.random.split(jax.random.key(seed), 15)
    inputs = scatter_about(arg_keys[0], (SLOTS, SEQS, D), 1.0, 6.0, ((0, 4), (1, 8)))
    cotangent = scatter_about(arg_keys[1], (SLOTS, SEQS, D), 1.0, 6.0, ((0, 4), (1, 8)))
    lengths = draw_lengths(jax.random.fold_in(arg_keys[14], 71), 0)
    block_order = draw_block_order(jax.random.fold_in(arg_keys[14], 71), 0)
    norm_gain = jnp.clip(1.0 + 0.1 * jax.random.normal(arg_keys[4], (D,), jnp.float32), 0.5, 1.5).astype(jnp.bfloat16)
    norm_bias = scatter_about(arg_keys[5], (D,), 0.3, 1.75, ((0, 8),))
    attend_weight = scatter_about(arg_keys[6], (D, 3 * D), D ** -0.5, 0.1875, ((0, 8),))
    attend_bias = scatter_about(arg_keys[7], (3 * D,), 0.5, 3.0, ((0, 8),))
    dense_weight = scatter_about(arg_keys[8], (D, D), (max(SLOTS // 512, 1)) ** -0.5, 6.0, ((0, 8),))
    dense_bias = scatter_about(arg_keys[9], (D,), 0.5, 3.0, ((0, 8),))
    up_weight = scatter_about(arg_keys[10], (D, FF), D ** -0.5, 0.1875, ((0, 8),))
    up_bias = scatter_about(arg_keys[11], (FF,), 0.5, 3.0, ((0, 8),))
    down_weight = scatter_about(arg_keys[12], (FF, D), FF ** -0.5, 0.09375, ((0, 8),))
    down_bias = scatter_about(arg_keys[13], (D,), 0.5, 3.0, ((0, 8),))
    return {"inputs": inputs, "cotangent": cotangent, "lengths": lengths, "block_order": block_order, "norm_gain": norm_gain, "norm_bias": norm_bias, "attend_weight": attend_weight, "attend_bias": attend_bias, "dense_weight": dense_weight, "dense_bias": dense_bias, "up_weight": up_weight, "up_bias": up_bias, "down_weight": down_weight, "down_bias": down_bias}


EPSILON = 1e-05
HIGHEST = lax.Precision.HIGHEST

@jax.custom_vjp
def low(v):
    return lax.optimization_barrier(v.astype(jnp.bfloat16)).astype(jnp.float32)

@jax.custom_vjp
def low_back(v):
    return v

def low_keep(v):
    return (low(v), None)

def low_pass(kept, grad):
    return (grad,)

def back_keep(v):
    return (v, None)

def back_low(kept, grad):
    return (low(grad),)
low.defvjp(low_keep, low_pass)
low_back.defvjp(back_keep, back_low)

def product(left, right):
    return jnp.dot(left, right, precision=HIGHEST, preferred_element_type=jnp.float32)

def angles(places):
    rates = 10000.0 ** (-jnp.arange(0, ROT, 2, dtype=jnp.float32) / ROT)
    turned = places.astype(jnp.float32)[:, None] * rates[None, :]
    doubled = jnp.concatenate([turned, turned], axis=-1)
    return (jnp.cos(doubled), jnp.sin(doubled))

def turn_half(values):
    half = values.shape[-1] // 2
    return jnp.concatenate([-values[..., half:], values[..., :half]], axis=-1)

def rotary(values, cosine, sine):
    front = values[..., :ROT]
    moved = front * cosine[None, :, None, :] + turn_half(front) * sine[None, :, None, :]
    return jnp.concatenate([moved, values[..., ROT:]], axis=-1)

def attend(queries, keys, values, places):
    groups, length = (queries.shape[0], queries.shape[1])
    rows = math.gcd(length, 512)
    count = length // rows
    scale = HEAD_DIM ** (-0.5)
    blocks = jnp.transpose(queries, (1, 0, 2, 3)).reshape(count, rows, groups, HEADS, HEAD_DIM)
    block_places = places.reshape(count, rows)

    def block(item):
        query_block, query_places = item
        scores = low_back(jnp.einsum('qghd,gkhd->ghqk', query_block, keys, precision=HIGHEST, preferred_element_type=jnp.float32) * scale)
        allowed = places[None, :] <= query_places[:, None]
        weights = jnp.where(allowed, jnp.exp(scores), 0.0)
        total = lax.optimization_barrier(jnp.sum(weights, axis=-1))
        summed = low_back(jnp.einsum('ghqk,gkhd->ghqd', low(weights), values, precision=HIGHEST, preferred_element_type=jnp.float32))
        return summed / total[..., None]
    mixed = lax.map(jax.checkpoint(block), (blocks, block_places))
    return jnp.transpose(mixed, (1, 0, 3, 2, 4)).reshape(groups, length, HEADS, HEAD_DIM)

def layer(inputs, tensors, valid, places):
    gain, shift, attend_full, attend_shift, dense_full, dense_shift, up_full, up_shift, down_full, down_shift = tensors
    groups, length, width = inputs.shape
    mean = lax.optimization_barrier(jnp.mean(inputs, axis=-1, keepdims=True))
    centred = inputs - mean
    inverse = lax.rsqrt(lax.optimization_barrier(jnp.mean(centred * centred, axis=-1, keepdims=True)) + EPSILON)
    normed_low = low(centred * inverse * gain + shift).reshape(groups * length, width)
    projected = low_back(product(normed_low, attend_full) + attend_shift).reshape(groups, length, 3, HEADS, HEAD_DIM)
    cosine, sine = angles(places)
    queries = low(rotary(projected[:, :, 0], cosine, sine))
    keys = low(rotary(projected[:, :, 1], cosine, sine))
    values = low(projected[:, :, 2])
    mixed_low = low(attend(queries, keys, values, places).reshape(groups * length, width))
    hidden = low_back(product(normed_low, up_full) + up_shift)
    active_low = low(jax.nn.gelu(hidden, approximate=False))
    branch = low_back(product(mixed_low, dense_full) + dense_shift + product(active_low, down_full) + down_shift)
    return valid[..., None] * (inputs + branch.reshape(groups, length, width))

def reference(inputs, cotangent, lengths, block_order, norm_gain, norm_bias, attend_weight, attend_bias, dense_weight, dense_bias, up_weight, up_bias, down_weight, down_bias):
    tensors = (norm_gain.astype(jnp.float32), norm_bias.astype(jnp.float32), attend_weight.astype(jnp.float32), attend_bias.astype(jnp.float32), dense_weight.astype(jnp.float32), dense_bias.astype(jnp.float32), up_weight.astype(jnp.float32), up_bias.astype(jnp.float32), down_weight.astype(jnp.float32), down_bias.astype(jnp.float32))
    slot_index = jnp.arange(SLOTS, dtype=jnp.int32)
    places = block_order[slot_index // BLK] * BLK + slot_index % BLK
    group = math.gcd(SEQS, max(1, 4096 // SLOTS))
    turns = SEQS // group
    seq_first = jnp.transpose(inputs.astype(jnp.float32), (1, 0, 2)).reshape(turns, group, SLOTS, D)
    pull_first = jnp.transpose(cotangent.astype(jnp.float32), (1, 0, 2)).reshape(turns, group, SLOTS, D)
    valid = (places[None, :] < lengths[:, None]).astype(jnp.float32).reshape(turns, group, SLOTS)

    def one_group(carry, item):
        source, pulled, valid_part = item

        def forward(source_in, tensors_in):
            return layer(source_in, tensors_in, valid_part, places)
        result, backward = jax.vjp(forward, source, tensors)
        grad_source, grad_tensors = backward(pulled)
        carry = tuple((left + right for left, right in zip(carry, grad_tensors)))
        return (carry, (result, grad_source))
    zeros = tuple((jnp.zeros_like(tensor) for tensor in tensors))
    totals, (results, grads) = lax.scan(one_group, zeros, (seq_first, pull_first, valid))
    output = jnp.transpose(results.reshape(SEQS, SLOTS, D), (1, 0, 2)).astype(jnp.bfloat16)
    input_grad = jnp.transpose(grads.reshape(SEQS, SLOTS, D), (1, 0, 2)).astype(jnp.bfloat16)
    return (output, input_grad, totals[0], totals[1], totals[2], totals[3], totals[4], totals[5], totals[6], totals[7], totals[8], totals[9])
```

```python
import functools

import jax
import jax.numpy as jnp
from jax import lax
from jax.experimental import pallas as pl
from jax.experimental.pallas import tpu as pltpu
from jax.sharding import PartitionSpec as P

HEADS = 16
HEAD_DIM = 64
ROT = 16
BLK = 64

EPSILON = 1e-05
ROOT_HALF = 0.7071067811865476
NORMAL_PEAK = 0.3989422804014327

F32 = jnp.float32
BF16 = jnp.bfloat16
SMEM = pltpu.MemorySpace.SMEM


def dot(left, right, dims):
    return lax.dot_general(left, right, ((dims[0], dims[1]), ((), ())), preferred_element_type=F32)


def matmul(left, right):
    return dot(left, right, ((1,), (0,)))


def matmul_rt(left, right):
    return dot(left, right, ((1,), (1,)))


def matmul_lt(left, right):
    return dot(left, right, ((0,), (0,)))


def at(array, index):
    return lax.dynamic_index_in_dim(array, index, 0, keepdims=False)


def swap(array, axis, mask):
    count = lax.axis_size(axis)
    return lax.ppermute(array, axis, [(i, i ^ mask) for i in range(count)])


def turn_z(array, step):
    count = lax.axis_size("dp")
    perm = [(i, (i + 2 * step) % count) for i in range(count)]
    return lax.ppermute(array, "dp", perm)


def gather_ctx(array):
    blocks = {0: array}
    mask = lax.axis_size("ctx") // 2
    while mask:
        for have in list(blocks):
            blocks[have ^ mask] = swap(blocks[have], "ctx", mask)
        mask //= 2
    return [blocks[m] for m in range(len(blocks))]


def scatter_ctx(chunks):
    held = dict(enumerate(chunks))
    mask = 1
    while mask < lax.axis_size("ctx"):
        for have in sorted(held):
            if have & mask == 0:
                got = swap(held[have ^ mask], "ctx", mask)
                held[have] = held[have].astype(F32) + got.astype(F32)
                if len(held) > 2:
                    held[have] = held[have].astype(BF16)
        held = {have: value for have, value in held.items() if have & mask == 0}
        mask *= 2
    return held[0]


def gather_small(array, axis):
    count = lax.axis_size(axis)
    index = lax.axis_index(axis)
    array = array[None]
    mask = 1
    while mask < count:
        got = swap(array, axis, mask)
        low = (index & mask) == 0
        array = jnp.concatenate(
            [jnp.where(low, array, got), jnp.where(low, got, array)], axis=0
        )
        mask *= 2
    return array


def sum_small(array, axis):
    mask = 1
    while mask < lax.axis_size(axis):
        array = array + swap(array, axis, mask)
        mask *= 2
    return array


def gather_dp(array):
    pieces = []
    current = array
    for k in range(lax.axis_size("dp") // 2):
        if k:
            current = turn_z(current, 1)
        pieces.append((current, swap(current, "dp", 1)))
    return pieces


def scatter_dp(block_of):
    count = lax.axis_size("dp") // 2
    index = lax.axis_index("dp")
    z, x = index // 2, index % 2
    total = None
    for s in range(1, count + 1):
        row = lax.rem(z - s + count, count)
        part = block_of(row, x).astype(F32) + swap(block_of(row, 1 - x), "dp", 1).astype(F32)
        if total is not None:
            part = part + turn_z(total, 1).astype(F32)
        total = part.astype(BF16)
    return total


def place_kernel(starts, *refs, axis, unit):
    *pieces, out = refs
    for i, piece in enumerate(pieces):
        start = pl.multiple_of(starts[i] * unit, unit)
        if axis == 0:
            out[pl.ds(start, piece.shape[0]), :] = piece[...].astype(out.dtype)
        else:
            out[:, pl.ds(start, piece.shape[1])] = piece[...].astype(out.dtype)


def place(pieces, starts, shape, axis, dtype, name):
    unit = pieces[0].shape[axis]
    size = sum(p.size * p.dtype.itemsize for p in pieces)
    whole = pl.BlockSpec(memory_space=pltpu.MemorySpace.VMEM)
    return pl.pallas_call(
        functools.partial(place_kernel, axis=axis, unit=unit),
        out_shape=jax.ShapeDtypeStruct(shape, dtype),
        in_specs=[pl.BlockSpec(memory_space=SMEM)] + [whole] * len(pieces),
        out_specs=whole,
        cost_estimate=pl.CostEstimate(flops=0, transcendentals=0, bytes_accessed=3 * size),
        name=name,
    )(starts, *pieces)


def attend_kernel(
    table,
    lengths,
    qkv_ref,
    pull_ref,
    cos_ref,
    up_ref,
    down_ref,
    mixed_ref,
    back_ref,
    q_s,
    k_s,
    v_s,
    pull_s,
    dk_s,
    dv_s,
    *,
    blocks,
    width,
    group,
    tile,
):
    seq = pl.program_id(0)
    length = lengths[seq]
    slots = blocks * BLK
    scale = HEAD_DIM ** (-0.5)
    lane = lax.broadcasted_iota(jnp.int32, (1, group), 1)
    masks = [(lane // HEAD_DIM) == h for h in range(group // HEAD_DIM)]
    row = lax.broadcasted_iota(jnp.int32, (tile, tile), 0)
    column = lax.broadcasted_iota(jnp.int32, (tile, tile), 1)
    allowed = column <= row

    def shifted(values, by):
        if group % 128 == 0:
            return pltpu.roll(values, by % group, 1)
        by = by % group
        return jnp.concatenate([values[:, group - by :], values[:, : group - by]], axis=1)

    def rotate(values, rows, sign):
        return values * cos_ref[rows, :] + sign * (
            shifted(values, ROT // 2) * up_ref[rows, :]
            + shifted(values, -(ROT // 2)) * down_ref[rows, :]
        )

    def stored(p):
        return pl.ds(pl.multiple_of(table[seq * blocks + p], BLK), BLK)

    def block_rows(p):
        return pl.ds(pl.multiple_of(p * BLK, BLK), BLK)

    for g in range(width // group):
        q_cols = slice(g * group, (g + 1) * group)
        k_cols = slice(width + g * group, width + (g + 1) * group)
        v_cols = slice(2 * width + g * group, 2 * width + (g + 1) * group)

        @pl.loop(0, blocks)
        def _(p):
            rows, here = stored(p), block_rows(p)
            q_s[here, :] = (rotate(qkv_ref[rows, q_cols], here, 1.0).astype(BF16).astype(F32) * scale).astype(BF16)
            k_s[here, :] = rotate(qkv_ref[rows, k_cols], here, 1.0).astype(BF16)
            v_s[here, :] = qkv_ref[rows, v_cols].astype(BF16)
            pull_s[here, :] = pull_ref[rows, q_cols]

        dk_s[...] = jnp.zeros_like(dk_s)
        dv_s[...] = jnp.zeros_like(dv_s)

        for i in range(slots // tile):
            top = slice(i * tile, (i + 1) * tile)

            @pl.when(i * tile < length)
            def _():
                q = q_s[top, :]
                pull = pull_s[top, :]
                mixed = jnp.zeros((tile, group), F32)
                dq = jnp.zeros((tile, group), F32)
                for mask in masks:
                    q_h = jnp.where(mask, q, jnp.zeros_like(q))
                    pull_h = jnp.where(mask, pull, 0.0)
                    weights = []
                    low = []
                    total = jnp.zeros((tile, 1), F32)
                    summed = jnp.zeros((tile, group), F32)
                    for j in range(i + 1):
                        cols = slice(j * tile, (j + 1) * tile)
                        w = jnp.exp(matmul_rt(q_h, k_s[cols, :]))
                        if j == i:
                            w = jnp.where(allowed, w, 0.0)
                        total = total + jnp.sum(w, axis=1, keepdims=True)
                        w_low = w.astype(BF16)
                        summed = summed + matmul(w_low, v_s[cols, :])
                        weights.append(w)
                        low.append(w_low)
                    inverse = 1.0 / total
                    mixed_h = jnp.where(mask, summed * inverse, 0.0)
                    mixed = mixed + mixed_h
                    scaled = (pull_h * inverse).astype(BF16)
                    correction = jnp.sum(pull_h * mixed_h, axis=1, keepdims=True) * inverse
                    part = jnp.zeros((tile, group), F32)
                    for j in range(i + 1):
                        cols = slice(j * tile, (j + 1) * tile)
                        pressure = matmul_rt(scaled, v_s[cols, :])
                        slopes = (weights[j] * (pressure - correction)).astype(BF16)
                        part = part + matmul(slopes, k_s[cols, :])
                        dk_s[cols, :] += matmul_lt(slopes, q_h)
                        dv_s[cols, :] += matmul_lt(low[j], scaled)
                    dq = dq + jnp.where(mask, part, 0.0)
                dq = rotate(dq * scale, top, -1.0).astype(BF16)
                mixed = mixed.astype(BF16)
                for b in range(tile // BLK):
                    rows = stored(i * tile // BLK + b)
                    mixed_ref[rows, q_cols] = mixed[b * BLK : (b + 1) * BLK]
                    back_ref[rows, q_cols] = dq[b * BLK : (b + 1) * BLK]

            @pl.when(i * tile >= length)
            def _():
                for b in range(tile // BLK):
                    rows = stored(i * tile // BLK + b)
                    zeros = jnp.zeros((BLK, group), BF16)
                    mixed_ref[rows, q_cols] = zeros
                    back_ref[rows, q_cols] = zeros

        @pl.loop(0, blocks)
        def _(p):
            rows, here = stored(p), block_rows(p)
            back_ref[rows, k_cols] = rotate(dk_s[here, :], here, -1.0).astype(BF16)
            back_ref[rows, v_cols] = dv_s[here, :].astype(BF16)


def attention(qkv, pull, table, lengths, tables, blocks):
    rows, width = pull.shape
    slots = blocks * BLK
    group = min(width, 128)
    tile = min(256, slots)
    sequences = lengths.shape[0]
    whole = pl.BlockSpec(memory_space=pltpu.MemorySpace.VMEM)
    pairs = sequences * (width // HEAD_DIM) * slots * slots
    return pl.pallas_call(
        functools.partial(attend_kernel, blocks=blocks, width=width, group=group, tile=tile),
        grid=(sequences,),
        out_shape=(
            jax.ShapeDtypeStruct((rows, width), BF16),
            jax.ShapeDtypeStruct((rows, 3 * width), BF16),
        ),
        in_specs=[pl.BlockSpec(memory_space=SMEM)] * 2 + [whole] * 5,
        out_specs=(whole, whole),
        scratch_shapes=[
            pltpu.VMEM((slots, group), BF16),
            pltpu.VMEM((slots, group), BF16),
            pltpu.VMEM((slots, group), BF16),
            pltpu.VMEM((slots, group), F32),
            pltpu.VMEM((slots, group), F32),
            pltpu.VMEM((slots, group), F32),
        ],
        compiler_params=pltpu.CompilerParams(
            dimension_semantics=("arbitrary",), vmem_limit_bytes=60 << 20
        ),
        cost_estimate=pl.CostEstimate(
            flops=pairs * HEAD_DIM * 14, transcendentals=pairs, bytes_accessed=rows * width * 30
        ),
        name="attend",
    )(table, lengths, qkv, pull, *tables)


def rotary_tables(slots, group):
    lane = jnp.arange(group, dtype=jnp.int32) % HEAD_DIM
    half = ROT // 2
    rates = 10000.0 ** (-jnp.arange(0, ROT, 2, dtype=F32) / ROT)
    turned = jnp.arange(slots, dtype=jnp.int32).astype(F32)[:, None] * rates[None, :]
    cosine, sine = jnp.cos(turned), jnp.sin(turned)
    rest = HEAD_DIM - ROT
    one = jnp.ones((slots, rest), F32)
    zero = jnp.zeros((slots, rest), F32)
    none = jnp.zeros((slots, half), F32)
    head_cos = jnp.concatenate([cosine, cosine, one], axis=1)
    head_up = jnp.concatenate([none, sine, zero], axis=1)
    head_down = jnp.concatenate([-sine, none, zero], axis=1)
    repeats = group // HEAD_DIM
    return tuple(jnp.concatenate([t] * repeats, axis=1) for t in (head_cos, head_up, head_down))


def body(
    inputs,
    cotangent,
    lengths,
    block_order,
    norm_gain,
    norm_bias,
    attend_weight,
    attend_bias,
    dense_weight,
    dense_bias,
    up_weight,
    up_bias,
    down_weight,
    down_bias,
):
    local, sequences, width = inputs.shape
    n_ctx, n_dp = lax.axis_size("ctx"), lax.axis_size("dp")
    c, d = lax.axis_index("ctx"), lax.axis_index("dp")
    z, x = d // 2, d % 2
    n_z = n_dp // 2
    rows = local * sequences
    slots = local * n_ctx
    blocks = slots // BLK
    own_blocks = local // BLK
    part = width // n_ctx
    hidden_width = up_weight.shape[1]
    shard = width // n_dp
    unit = hidden_width // (n_dp * n_ctx)

    sizes = [
        norm_gain.shape[0],
        norm_bias.shape[0],
        dense_bias.shape[0],
        down_bias.shape[0],
        up_bias.shape[0],
        attend_bias.shape[0],
    ]
    short = gather_small(
        jnp.concatenate([norm_gain, norm_bias, dense_bias, down_bias, up_bias, attend_bias]), "dp"
    ).astype(F32)
    ends = [sum(sizes[:i]) for i in range(len(sizes) + 1)]
    gain, shift, dense_shift, down_shift, up_shift, attend_shift = (
        short[:, ends[i] : ends[i + 1]] for i in range(len(sizes))
    )
    gain, shift, dense_shift, down_shift = (
        t.reshape(width) for t in (gain, shift, dense_shift, down_shift)
    )
    up_shift = at(jnp.moveaxis(up_shift.reshape(n_dp, n_ctx, unit), 1, 0), c).reshape(n_dp * unit)
    attend_shift = at(jnp.moveaxis(attend_shift.reshape(3, n_ctx, part), 1, 0), c).reshape(3 * part)

    attend_mine = lax.dynamic_index_in_dim(
        attend_weight.reshape(shard, 3, n_ctx, part), c, 2, keepdims=False
    ).reshape(shard, 3 * part)
    dense_mine = lax.dynamic_slice_in_dim(dense_weight, c * part, part, 1)
    up_mine = lax.dynamic_index_in_dim(
        up_weight.reshape(shard, n_dp, n_ctx, unit), c, 2, keepdims=False
    ).reshape(shard, n_dp * unit)
    down_mine = lax.dynamic_slice_in_dim(down_weight, c * unit, unit, 0)

    steps = jnp.arange(n_z, dtype=jnp.int32)
    origin = lax.rem(z - steps + n_z, n_z) * 2
    dp_starts = jnp.stack([origin + x, origin + 1 - x], axis=1).reshape(n_dp)

    def weight_dp(mine, name):
        pieces = [p for pair in gather_dp(mine) for p in pair]
        shape = (mine.shape[0] * n_dp, mine.shape[1])
        return place(pieces, dp_starts, shape, 0, BF16, name)

    first = weight_dp(jnp.concatenate([attend_mine, dense_mine], axis=1), "place_first")
    attend_c = first[:, : 3 * part]
    ctx_starts = c ^ jnp.arange(n_ctx, dtype=jnp.int32)
    dense_by_owner = first[:, 3 * part :].reshape(n_ctx, part, part)
    dense_pieces = [at(dense_by_owner, c)] + [
        swap(at(dense_by_owner, c ^ m), "ctx", m) for m in range(1, n_ctx)
    ]
    if part % 128 == 0:
        dense_c = place(dense_pieces, ctx_starts, (part, width), 1, BF16, "place_dense")
    else:
        dense_stack = jnp.stack(dense_pieces)
        dense_c = jnp.concatenate([at(dense_stack, c ^ j) for j in range(n_ctx)], axis=1)
    up_c = weight_dp(up_mine, "place_up")
    down_c = weight_dp(down_mine, "place_down")

    slot = c * local + jnp.arange(local, dtype=jnp.int32)
    chosen = jnp.sum(
        jnp.where(
            (slot // BLK)[:, None] == jnp.arange(blocks, dtype=jnp.int32)[None, :],
            block_order[None, :],
            0,
        ),
        axis=1,
    )
    places = chosen * BLK + slot % BLK
    valid = (places[None, :] < lengths[:, None]).astype(F32).reshape(rows, 1)
    source = jnp.transpose(inputs, (1, 0, 2)).reshape(rows, width).astype(F32)
    pulled = valid * jnp.transpose(cotangent, (1, 0, 2)).reshape(rows, width).astype(F32)
    mean = jnp.mean(source, axis=-1, keepdims=True)
    centred = source - mean
    inverse = lax.rsqrt(jnp.mean(centred * centred, axis=-1, keepdims=True) + EPSILON)
    unit_rows = centred * inverse
    normed_own = (unit_rows * gain + shift).astype(BF16)
    pulled_own = pulled.astype(BF16)
    normed = jnp.concatenate(gather_ctx(normed_own), axis=0)
    pulled_low = jnp.concatenate(gather_ctx(pulled_own), axis=0)

    table_index = jnp.arange(blocks, dtype=jnp.int32)
    stored = jnp.sum(
        jnp.where(block_order[None, :] == table_index[:, None], table_index[None, :], 0), axis=1
    )
    starts = ((stored // own_blocks) ^ c) * rows + (stored % own_blocks) * BLK
    table = (starts[None, :] + jnp.arange(sequences, dtype=jnp.int32)[:, None] * local).reshape(-1)

    qkv = matmul(normed, attend_c) + attend_shift
    back_mixed = matmul_rt(pulled_low, dense_c)
    mixed_low, back_projected = attention(
        qkv,
        back_mixed,
        table.astype(jnp.int32),
        lengths,
        rotary_tables(slots, min(part, 128)),
        blocks,
    )

    grad_dense = matmul_lt(mixed_low, pulled_low).astype(BF16)
    grad_attend = matmul_lt(normed, back_projected).astype(BF16)
    dense_grad_cols = jnp.moveaxis(grad_dense.reshape(part, n_ctx, part), 1, 0)
    dense_grad_pieces = [at(dense_grad_cols, c)] + [
        swap(at(dense_grad_cols, c ^ m), "ctx", m) for m in range(1, n_ctx)
    ]
    dense_grad = place(dense_grad_pieces, ctx_starts, (width, part), 0, BF16, "place_dense_grad")

    hidden = matmul(normed, up_c) + up_shift
    phi = 0.5 * (1.0 + lax.erf(hidden * ROOT_HALF))
    active = (hidden * phi).astype(BF16)
    slope = phi + hidden * jnp.exp(-0.5 * hidden * hidden) * NORMAL_PEAK
    back_hidden = (matmul_rt(pulled_low, down_c) * slope).astype(BF16)
    grad_down = matmul_lt(active, pulled_low).astype(BF16)
    grad_up = matmul_lt(normed, back_hidden).astype(BF16)

    back_normed = (matmul_rt(back_projected, attend_c) + matmul_rt(back_hidden, up_c)).astype(BF16)
    branch = (matmul(mixed_low, dense_c) + matmul(active, down_c)).astype(BF16)

    def blocks_of(array):
        cut = array.reshape(n_dp, array.shape[0] // n_dp, array.shape[1])
        return lambda row, col: at(cut, row * 2 + col)

    attend_sum = scatter_dp(blocks_of(grad_attend))
    dense_sum = scatter_dp(blocks_of(dense_grad))
    down_sum = scatter_dp(blocks_of(grad_down))
    up_sum = scatter_dp(blocks_of(grad_up))

    def by_owner(shards):
        stack = jnp.stack(shards)
        return [at(stack, c ^ j).astype(F32) for j in range(n_ctx)]

    attend_out = jnp.stack(
        [t.reshape(shard, 3, part) for t in by_owner(gather_ctx(attend_sum))], axis=2
    ).reshape(shard, 3 * width)
    dense_out = jnp.concatenate(by_owner(gather_ctx(dense_sum)), axis=1)
    down_out = jnp.concatenate(by_owner(gather_ctx(down_sum)), axis=0)
    up_out = jnp.stack(
        [t.reshape(shard, n_dp, unit) for t in by_owner(gather_ctx(up_sum))], axis=2
    ).reshape(shard, hidden_width)

    def chunks(array):
        return [array[m * rows : (m + 1) * rows] for m in range(n_ctx)]

    branch_own = scatter_ctx(chunks(branch)) + dense_shift + down_shift
    output = (valid * (source + branch_own)).astype(BF16)
    back_own = scatter_ctx(chunks(back_normed))
    back_unit = back_own * gain
    back_source = inverse * (
        back_unit
        - jnp.mean(back_unit, axis=-1, keepdims=True)
        - unit_rows * jnp.mean(back_unit * unit_rows, axis=-1, keepdims=True)
    )
    input_grad = (pulled + back_source).astype(BF16)

    def to_slots(array):
        return jnp.transpose(array.reshape(sequences, local, width), (1, 0, 2))

    mine = (jnp.arange(n_ctx, dtype=jnp.int32) == c).astype(F32)
    attend_short = jnp.sum(back_projected.astype(F32), axis=0).reshape(3, 1, part)
    up_short = jnp.sum(back_hidden.astype(F32), axis=0).reshape(n_dp, 1, unit)
    short_grads = jnp.concatenate(
        [
            jnp.sum(back_own * unit_rows, axis=0).reshape(n_dp, shard),
            jnp.sum(back_own, axis=0).reshape(n_dp, shard),
            jnp.sum(pulled_own.astype(F32), axis=0).reshape(n_dp, shard),
            (attend_short * mine[None, :, None]).reshape(n_dp, 3 * shard),
            (up_short * mine[None, :, None]).reshape(n_dp, n_ctx * unit),
        ],
        axis=1,
    )
    short_sum = at(sum_small(sum_small(short_grads, "dp"), "ctx"), d)
    grad_gain = short_sum[:shard]
    grad_shift = short_sum[shard : 2 * shard]
    grad_bias = short_sum[2 * shard : 3 * shard]
    grad_attend_bias = short_sum[3 * shard : 6 * shard]
    grad_up_bias = short_sum[6 * shard :]

    return (
        to_slots(output),
        to_slots(input_grad),
        grad_gain,
        grad_shift,
        attend_out,
        grad_attend_bias,
        dense_out,
        grad_bias,
        up_out,
        grad_up_bias,
        down_out,
        grad_bias,
    )


def solution(mesh):
    row, flat, wide = P("ctx", "dp", None), P("dp"), P("dp", None)
    return jax.shard_map(
        body,
        mesh=mesh,
        in_specs=(row, row, flat, P(), flat, flat, wide, flat, wide, flat, wide, flat, wide, flat),
        out_specs=(row, row, flat, flat, wide, flat, wide, flat, wide, flat, wide, flat),
        check_vma=False,
    )
```
